32 devices in a mesh: slot: 8 (over z, x), grp: 4 (over y, core).
Axes of the slice: x: 2, y: 2, z: 4, core: 2. Of those that a mesh axis runs over, the one named last changes fastest.
Arguments:
- token_rows: bfloat16 [2, 8, 4, 384, 2048], P(None, 'slot', 'grp'), may hold values from -6 to 6
- cotangents: bfloat16 [2, 8, 4, 384, 2048], P(None, 'slot', 'grp'), may hold values from -6 to 6
- row_counts: int32 [2, 8, 4], P(None, 'slot', 'grp'), may hold values from 96 to 384, as said below
- old_place: int32 [8, 4], replicated, may hold values from 0 to 3, as said below
- new_place: int32 [8, 4], replicated, may hold values from 0 to 3, as said below
- momentum: float32 [16, 3145728], P(None, ('slot', 'grp')), may hold values from -4 to 4
- curvature: float32 [16, 3145728], P(None, ('slot', 'grp')), may hold values from 0.01 to 1
- master: float32 [16, 3145728], P(None, ('slot', 'grp')), may hold values from -0.125 to 0.125
Outputs:
- d_rows: bfloat16 [2, 8, 4, 384, 2048], P(None, 'slot', 'grp')
- momentum_out: float32 [16, 3145728], P(None, ('slot', 'grp'))
- curvature_out: float32 [16, 3145728], P(None, ('slot', 'grp'))
- master_out: float32 [16, 3145728], P(None, ('slot', 'grp'))
The draws below stay inside these ranges and needn't reach their ends.
Inputs may be any that keep to these rules, and one draw needn't show every extreme that they name: `old_place`: entry [s, g] is the expert, numbered within group g, held by slot s of group g; each of the 4 experts of every group has at least one slot. `new_place`: entry [s, g] is the expert, numbered within group g, held by slot s of group g; each of the 4 experts of every group has at least one slot. `row_counts`: rows from this count on are padding; in each step some slot has exactly 384 live rows.
All inputs are finite; a program needn't handle non-finite values.
Results may differ from the reference program's by a relative error of at most 0.0074.
Values may be sent and summed in bfloat16 or wider, within the bound.
A program may use at most 128 MiB of HBM per device.

```python
import math
import jax
import jax.numpy as jnp
from jax import lax

D = 2048
FF = 512
CAP = 384
EXP_GRP = 4
STEPS = 2
SLOTS = 8
GROUPS = 4
EXPERTS = 16
PARAMS = 3145728


def place_draw(key):
    key_list = jax.random.split(key, 3)
    slot_order = jax.vmap(lambda subkey: jax.random.permutation(subkey, SLOTS))(jax.random.split(key_list[0], GROUPS))
    expert_order = jax.vmap(lambda subkey: jax.random.permutation(subkey, EXP_GRP))(jax.random.split(key_list[1], GROUPS))
    slot_rank = jnp.argsort(slot_order, axis=1).astype(jnp.int32)
    tickets = jax.random.randint(key_list[2], (GROUPS, SLOTS), 0, 2 ** EXP_GRP - 1)
    bounds = 2 ** jnp.arange(1, EXP_GRP, dtype=jnp.int32) - 1
    tier_index = jnp.sum((tickets[:, :, None] >= bounds[None, None, :]).astype(jnp.int32), axis=2)
    drawn_expert = jnp.take_along_axis(expert_order, tier_index, axis=1)
    fixed_expert = jnp.take_along_axis(expert_order, jnp.minimum(slot_rank, EXP_GRP - 1), axis=1)
    chosen = jnp.where(slot_rank < EXP_GRP, fixed_expert, drawn_expert)
    return chosen.T.astype(jnp.int32)


def draw_old_place(key, part):
    return place_draw(jax.random.fold_in(key, 11))


def draw_new_place(key, part):
    return place_draw(jax.random.fold_in(key, 12))


def draw_row_counts(key, part):
    first, second = jax.random.split(jax.random.fold_in(key, 31))
    counts = jax.random.randint(first, (STEPS, SLOTS * GROUPS), CAP // 4, CAP + 1)
    full_slot = jax.random.randint(second, (STEPS, 1), 0, SLOTS * GROUPS)
    chosen = jnp.arange(SLOTS * GROUPS, dtype=jnp.int32)[None, :] == full_slot
    return jnp.where(chosen, CAP, counts).reshape(STEPS, SLOTS, GROUPS).astype(jnp.int32)


def block_scale(key, extent, pieces, smallest, high):
    loudness = 1.0
    for dim, parts in pieces:
        steps = jax.random.uniform(jax.random.fold_in(jax.random.fold_in(key, 6), dim), (parts,), jnp.float32, smallest / len(pieces), high / len(pieces))
        loudness = loudness * jnp.repeat(jnp.exp(steps), extent[dim] // parts).reshape((-1,) + (1,) * (len(extent) - 1 - dim))
    return loudness


def normal_values(stream_key, shape, spread, limit, cuts=(), kind=jnp.bfloat16):
    drawn = jax.random.normal(stream_key, shape, jnp.float32) * spread
    if len(cuts) > 0:
        drawn = block_scale(stream_key, shape, cuts, -0.22, 0.18) * drawn
    return jnp.clip(drawn, min=-limit, max=limit).astype(kind)


def setup_inputs(seed: int = 0) -> dict:
    splits = jax.random.split(jax.random.key(seed), 9)
    token_rows = normal_values(splits[0], (STEPS, SLOTS, GROUPS, CAP, D), 1.0, 6.0, ((1, 8), (2, 4)))
    cotangents = normal_values(splits[1], (STEPS, SLOTS, GROUPS, CAP, D), 1.0, 6.0, ((1, 8), (2, 4)))
    row_counts = draw_row_counts(jax.random.fold_in(splits[8], 71), 0)
    old_place = draw_old_place(jax.random.fold_in(splits[8], 71), 0)
    new_place = draw_new_place(jax.random.fold_in(splits[8], 71), 0)
    momentum = normal_values(splits[5], (EXPERTS, PARAMS), 0.5, 4.0, ((1, 32),), jnp.float32)
    curvature = jnp.clip(jnp.exp(math.log(1.0) - 4.6051702 * jax.random.uniform(splits[6], (EXPERTS, PARAMS), jnp.float32) ** block_scale(splits[6], (EXPERTS, PARAMS), ((1, 32),), -0.2, 0.2)), 0.01, 1.0)
    master = normal_values(splits[7], (EXPERTS, PARAMS), D ** -0.5, 0.125, ((1, 32),), jnp.float32)
    return {"token_rows": token_rows, "cotangents": cotangents, "row_counts": row_counts, "old_place": old_place, "new_place": new_place, "momentum": momentum, "curvature": curvature, "master": master}


beta_one = 0.9
beta_two = 0.99
rho_scale = 2.0
learn_rate = 0.005
grad_scale = 0.25


def silu_parts(values):
    sigmoid = jax.nn.sigmoid(values)
    return values * sigmoid, sigmoid * (1.0 + values * (1.0 - sigmoid))


def slot_backward(rows_one, cotangent, live_count, flat_weights):
    split_at = 2 * D * FF
    w_gateup = flat_weights[:split_at].reshape(D, 2 * FF)
    w_down = flat_weights[split_at:].reshape(FF, D)
    live = (jnp.arange(rows_one.shape[0], dtype=jnp.int32) < live_count)[:, None]
    masked_ct = jnp.where(live, cotangent, jnp.zeros_like(cotangent))
    preact = jnp.dot(rows_one, w_gateup, preferred_element_type=jnp.float32)
    gate_pre = preact[:, :FF]
    up_pre = preact[:, FF:]
    activated, slope = silu_parts(gate_pre)
    hidden = (activated * up_pre).astype(jnp.bfloat16)
    hidden_grad = lax.dot_general(masked_ct, w_down, (((1,), (1,)), ((), ())), preferred_element_type=jnp.float32)
    pre_grad = jnp.concatenate([hidden_grad * up_pre * slope, hidden_grad * activated], axis=1).astype(jnp.bfloat16)
    row_grad = lax.dot_general(pre_grad, w_gateup, (((1,), (1,)), ((), ())), preferred_element_type=jnp.float32).astype(jnp.bfloat16)
    grad_gateup = lax.dot_general(rows_one, pre_grad, (((0,), (0,)), ((), ())), preferred_element_type=jnp.float32)
    grad_down = lax.dot_general(hidden, masked_ct, (((0,), (0,)), ((), ())), preferred_element_type=jnp.float32)
    return row_grad, jnp.concatenate([grad_gateup.reshape(-1), grad_down.reshape(-1)])


def sophia(grads, momentum, curvature, master):
    momentum = beta_one * momentum + (1.0 - beta_one) * grads
    curvature = beta_two * curvature + (1.0 - beta_two) * grads * grads
    master = master - learn_rate * jnp.clip(momentum / (rho_scale * curvature), -1.0, 1.0)
    return momentum, curvature, master


def reference(token_rows, cotangents, row_counts, old_place, new_place, momentum, curvature, master):
    owners = (jnp.arange(GROUPS, dtype=jnp.int32) * EXP_GRP)[None, :]
    outputs = []
    for step_index, place_map in ((0, old_place), (1, new_place)):
        expert_ids = (place_map + owners).reshape(-1).astype(jnp.int32)
        weights_bf = master.astype(jnp.bfloat16)
        rows_all = token_rows[step_index].reshape(SLOTS * GROUPS, CAP, D)
        ct_all = cotangents[step_index].reshape(SLOTS * GROUPS, CAP, D)
        counts_all = row_counts[step_index].reshape(-1)

        def per_slot(totals, items):
            rows_one, ct_one, count_one, expert_one = items
            flat = lax.dynamic_index_in_dim(weights_bf, expert_one, 0, keepdims=False)
            row_grad, flat_grad = slot_backward(rows_one, ct_one, count_one, flat)
            current = lax.dynamic_index_in_dim(totals, expert_one, 0, keepdims=False)
            totals = lax.dynamic_update_index_in_dim(totals, current + flat_grad, expert_one, 0)
            return totals, row_grad

        totals, row_grads = lax.scan(per_slot, jnp.zeros((EXPERTS, PARAMS), jnp.float32), (rows_all, ct_all, counts_all, expert_ids))
        momentum, curvature, master = sophia(totals * grad_scale, momentum, curvature, master)
        outputs.append(row_grads.reshape(SLOTS, GROUPS, CAP, D))
    return jnp.stack(outputs), momentum, curvature, master
```

```python
import functools

import jax
import jax.numpy as jnp
from jax import lax
from jax.experimental import pallas as pl
from jax.experimental.pallas import tpu as pltpu
from jax.sharding import PartitionSpec as P

D = 2048
FF = 512
WIDE = 2 * FF
LANES = 128
CHUNKS = 3


beta_one = 0.9
beta_two = 0.99
rho_scale = 2.0
learn_rate = 0.005
grad_scale = 0.25


def silu_parts(values):
    sigmoid = jax.nn.sigmoid(values)
    return (values * sigmoid, sigmoid * (1.0 + values * (1.0 - sigmoid)))


def slot_backward(rows_one, cotangent, live_count, weight_rows):
    w_gateup = weight_rows[:D]
    w_down = weight_rows[D:].reshape(FF, D)
    live = (jnp.arange(rows_one.shape[0], dtype=jnp.int32) < live_count)[:, None]
    masked_ct = jnp.where(live, cotangent, jnp.zeros_like(cotangent))
    preact = jnp.dot(rows_one, w_gateup, preferred_element_type=jnp.float32)
    gate_pre = preact[:, :FF]
    up_pre = preact[:, FF:]
    activated, slope = silu_parts(gate_pre)
    hidden = (activated * up_pre).astype(jnp.bfloat16)
    hidden_grad = lax.dot_general(
        masked_ct, w_down, (((1,), (1,)), ((), ())), preferred_element_type=jnp.float32
    )
    pre_grad = jnp.concatenate(
        [hidden_grad * up_pre * slope, hidden_grad * activated], axis=1
    ).astype(jnp.bfloat16)
    grad_gateup = lax.dot_general(
        rows_one, pre_grad, (((0,), (0,)), ((), ())), preferred_element_type=jnp.float32
    ).astype(jnp.bfloat16)
    grad_down = lax.dot_general(
        hidden, masked_ct, (((0,), (0,)), ((), ())), preferred_element_type=jnp.float32
    ).astype(jnp.bfloat16)
    row_grad = lax.dot_general(
        pre_grad, w_gateup, (((1,), (1,)), ((), ())), preferred_element_type=jnp.float32
    ).astype(jnp.bfloat16)
    return row_grad, jnp.concatenate([grad_gateup, grad_down.reshape(-1, WIDE)])


def pack_out(experts, rows, ids_ref, staged, out_ref):
    span = experts * rows

    def one(dest, carry):
        base = ids_ref[dest] * rows
        for lane in range(WIDE // LANES):
            piece = staged[pl.ds(pl.multiple_of(lane * span + base, 8), rows), :]
            out_ref[dest, :, lane * LANES:(lane + 1) * LANES] = piece.astype(jnp.bfloat16)
        return carry

    lax.fori_loop(0, out_ref.shape[0], one, 0)


def pack_kernel(experts, rows, ids_ref, w_ref, out_ref, staged):
    span = experts * rows
    for row in range(rows):
        for lane in range(WIDE // LANES):
            at = row * WIDE + lane * LANES
            staged[pl.ds(lane * span + row, experts, stride=rows), :] = w_ref[:, at:at + LANES]
    pack_out(experts, rows, ids_ref, staged, out_ref)


def sophia_kernel(experts, rows, packs, kept, *refs):
    ids_ref, next_ref, got_ref, m_ref, c_ref, w_ref = refs[:6]
    refs = refs[6 + kept:]
    m_out, c_out, w_out = refs[:3]
    total = refs[-1]
    span = experts * rows
    total[...] = jnp.zeros_like(total)

    def add(source, carry):
        base = ids_ref[source] * rows
        for lane in range(WIDE // LANES):
            at = pl.ds(pl.multiple_of(lane * span + base, 8), rows)
            piece = got_ref[source, :, lane * LANES:(lane + 1) * LANES]
            total[at, :] = total[at, :] + piece.astype(jnp.float32)
        return carry

    lax.fori_loop(0, got_ref.shape[0], add, 0)
    for row in range(rows):
        for lane in range(WIDE // LANES):
            at = pl.ds(lane * span + row, experts, stride=rows)
            cols = pl.ds(row * WIDE + lane * LANES, LANES)
            grads = total[at, :] * grad_scale
            moment = beta_one * m_ref[:, cols] + (1.0 - beta_one) * grads
            curve = beta_two * c_ref[:, cols] + (1.0 - beta_two) * grads * grads
            weight = w_ref[:, cols] - learn_rate * jnp.clip(
                moment / (rho_scale * curve), -1.0, 1.0
            )
            m_out[:, cols] = moment
            c_out[:, cols] = curve
            w_out[:, cols] = weight
            if packs:
                total[at, :] = weight
    if packs:
        pack_out(experts, rows, next_ref, total, refs[3])


def block_rows(chunk_rows):
    return 16 if chunk_rows % 16 == 0 else chunk_rows


def pack_chunk(chunk, chunk_rows, ids, master):
    experts, devices = master.shape[0], ids.shape[0]
    rows = block_rows(chunk_rows)
    steps = chunk_rows // rows
    return pl.pallas_call(
        functools.partial(pack_kernel, experts, rows),
        grid_spec=pltpu.PrefetchScalarGridSpec(
            num_scalar_prefetch=1,
            grid=(steps,),
            in_specs=[pl.BlockSpec((experts, rows * WIDE), lambda i, *_: (0, chunk * steps + i))],
            out_specs=pl.BlockSpec((devices, rows, WIDE), lambda i, *_: (0, i, 0)),
            scratch_shapes=[pltpu.VMEM((WIDE // LANES * experts * rows, LANES), jnp.float32)],
        ),
        out_shape=jax.ShapeDtypeStruct((devices, chunk_rows, WIDE), jnp.bfloat16),
        name="pack",
    )(ids, master)


def sophia_chunk(chunk, chunk_rows, ids, next_ids, got, state, whole, final):
    experts, devices = state[0].shape[0], ids.shape[0]
    rows = block_rows(chunk_rows)
    steps = chunk_rows // rows
    shift = chunk * steps
    kept = 0 if whole is None else 3
    near = pl.BlockSpec((experts, rows * WIDE), lambda i, *_: (0, i))
    far = pl.BlockSpec((experts, rows * WIDE), lambda i, *_: (0, shift + i))
    packed = pl.BlockSpec((devices, rows, WIDE), lambda i, *_: (0, i, 0))
    width = chunk_rows * WIDE * (CHUNKS if final else 1)
    out_shape = [jax.ShapeDtypeStruct((experts, width), jnp.float32)] * 3
    out_specs = [far if final else near] * 3
    if not final:
        out_shape = out_shape + [jax.ShapeDtypeStruct((devices, chunk_rows, WIDE), jnp.bfloat16)]
        out_specs = out_specs + [packed]
    return pl.pallas_call(
        functools.partial(sophia_kernel, experts, rows, not final, kept),
        grid_spec=pltpu.PrefetchScalarGridSpec(
            num_scalar_prefetch=2,
            grid=(steps,),
            in_specs=[packed]
            + [near if final else far] * 3
            + [pl.BlockSpec(memory_space=pl.ANY)] * kept,
            out_specs=out_specs,
            scratch_shapes=[pltpu.VMEM((WIDE // LANES * experts * rows, LANES), jnp.float32)],
        ),
        out_shape=out_shape,
        input_output_aliases={6 + i: i for i in range(kept)},
        name="sophia",
    )(ids, next_ids, got, *state, *(whole or ()))


def body(token_rows, cotangents, row_counts, old_place, new_place, momentum, curvature, master):
    group_count = lax.axis_size("grp")
    slot_count = lax.axis_size("slot")
    device_count = group_count * slot_count
    experts = master.shape[0]
    per_group = experts // group_count
    chunk_rows = master.shape[1] // (CHUNKS * WIDE)
    owners = (jnp.arange(group_count, dtype=jnp.int32) * per_group)[None, :]
    ids = [(place + owners).reshape(-1) for place in (old_place, new_place)]

    def swap(array):
        return lax.all_to_all(array, ("slot", "grp"), split_axis=0, concat_axis=0, tiled=True)

    arrived = [swap(pack_chunk(k, chunk_rows, ids[0], master)) for k in range(CHUNKS)]
    outputs = []
    states = [(momentum, curvature, master)] * CHUNKS
    whole = None
    for step_index in range(2):
        final = step_index == 1
        weight_rows = jnp.stack(arrived, axis=1).reshape(-1, WIDE)
        row_grad, grad_rows = slot_backward(
            token_rows[step_index, 0, 0],
            cotangents[step_index, 0, 0],
            row_counts[step_index, 0, 0],
            weight_rows,
        )
        outputs.append(row_grad)
        grad_rows = grad_rows.reshape(device_count, CHUNKS, chunk_rows, WIDE)
        got = [swap(grad_rows[:, k]) for k in range(CHUNKS)]
        arrived = []
        for k in range(CHUNKS):
            result = sophia_chunk(
                k, chunk_rows, ids[step_index], ids[1], got[k], states[k], whole, final
            )
            if final:
                whole = tuple(result)
            else:
                states[k] = tuple(result[:3])
                arrived.append(swap(result[3]))
    return (jnp.stack(outputs)[:, None, None], *whole)


def solution(mesh):
    return jax.shard_map(
        body,
        mesh=mesh,
        in_specs=(
            P(None, "slot", "grp", None, None),
            P(None, "slot", "grp", None, None),
            P(None, "slot", "grp"),
            P(),
            P(),
            P(None, ("slot", "grp")),
            P(None, ("slot", "grp")),
            P(None, ("slot", "grp")),
        ),
        out_specs=(
            P(None, "slot", "grp", None, None),
            P(None, ("slot", "grp")),
            P(None, ("slot", "grp")),
            P(None, ("slot", "grp")),
        ),
        check_vma=False,
    )
```

```python
import functools

import jax
import jax.numpy as jnp
from jax import lax
from jax.experimental import pallas as pl
from jax.experimental.pallas import tpu as pltpu
from jax.sharding import PartitionSpec as P

D = 2048
FF = 512
WIDE = 2 * FF
LANES = 128
TILE = 256
CHUNKS = 3
FIRST = ((0, 1), (1, 2))
REST = ((0, 2), (2, 1))


beta_one = 0.9
beta_two = 0.99
rho_scale = 2.0
learn_rate = 0.005
grad_scale = 0.25


def silu_parts(values):
    sigmoid = jax.nn.sigmoid(values)
    return (values * sigmoid, sigmoid * (1.0 + values * (1.0 - sigmoid)))


def contract(left, right, dims):
    return lax.dot_general(left, right, ((dims[:1], dims[1:]), ((), ())), preferred_element_type=jnp.float32)


def move_rows(spans, unit, chunk_refs, whole, sem, inward):
    share = whole.shape[0] // chunk_refs[0].shape[0]
    for (start, count), ref in zip(spans, chunk_refs):
        rows = count * unit

        def one(device, carry):
            part = whole.at[pl.ds(pl.multiple_of(device * share + start * unit, 8), rows), :]
            ends = (ref.at[device], part) if inward else (part, ref.at[device])
            pltpu.make_async_copy(*ends, sem).start()
            return carry

        lax.fori_loop(0, ref.shape[0], one, 0)


def spread(half):
    row = lax.broadcasted_iota(jnp.int32, (TILE // 2, TILE), 0)
    column = lax.broadcasted_iota(jnp.int32, (TILE // 2, TILE), 1)
    return jnp.where(column == 2 * row + half, 1.0, 0.0).astype(jnp.bfloat16)


def tiles(extent, size, step):
    def one(index, carry):
        step(pl.ds(pl.multiple_of(index * size, size), size), index)
        return carry

    lax.fori_loop(0, extent // size, one, 0)


def slot_kernel(spans_in, spans_out, unit, count_ref, x_ref, ct_ref, *refs):
    n_in, n_out = len(spans_in), len(spans_out)
    arrived, refs = refs[:n_in], refs[n_in:]
    grads_out, refs = refs[:n_out], refs[n_out:]
    dz, weights, grads, masked, preact, halves, hidden, hidden_up, sem = refs
    move_rows(spans_in, unit, arrived, weights, sem.at[0], True)
    live_count = count_ref[0]

    def mask(at, index):
        values = ct_ref[at, :].astype(jnp.float32)
        row = index * 16 + lax.broadcasted_iota(jnp.int32, values.shape, 0)
        masked[at, :] = jnp.where(row < live_count, values, 0.0).astype(jnp.bfloat16)

    tiles(ct_ref.shape[0], 16, mask)
    pltpu.make_async_copy(weights, weights, sem.at[0]).wait()

    def forward(at, index):
        preact[:, at] = contract(x_ref[...], weights[:D, at], (1, 0))

    tiles(WIDE, TILE, forward)

    def split(at, index):
        part = weights[pl.ds(pl.multiple_of(D + index * TILE, TILE), TILE), :]
        to = pl.ds(pl.multiple_of(index * (TILE // 2), TILE // 2), TILE // 2)
        for half in range(2):
            halves[half, to, :] = contract(spread(half), part, (1, 0)).astype(jnp.bfloat16)

    tiles(WIDE, TILE, split)

    def backward(at, index):
        hidden_grad = contract(masked[:, :WIDE], halves[0, at, :], (1, 1))
        hidden_grad = hidden_grad + contract(masked[:, WIDE:], halves[1, at, :], (1, 1))
        up_at = pl.ds(pl.multiple_of(FF + index * TILE, TILE), TILE)
        up_pre = preact[:, up_at]
        activated, slope = silu_parts(preact[:, at])
        hidden[:, at] = (activated * up_pre).astype(jnp.bfloat16)
        dz[:, at] = (hidden_grad * up_pre * slope).astype(jnp.bfloat16)
        dz[:, up_at] = (hidden_grad * activated).astype(jnp.bfloat16)

    tiles(FF, TILE, backward)

    def widen(at, index):
        part = hidden[:, pl.ds(pl.multiple_of(index * (TILE // 2), TILE // 2), TILE // 2)]
        for half in range(2):
            hidden_up[half, :, at] = contract(part, spread(half), (1, 0)).astype(jnp.bfloat16)

    tiles(WIDE, TILE, widen)

    def gateup(at, index):
        grads[at, :] = contract(x_ref[:, at], dz[...], (0, 0)).astype(jnp.bfloat16)

    tiles(D, TILE, gateup)

    def down(at, index):
        total = contract(hidden_up[0, :, at], masked[:, :WIDE], (0, 0))
        total = total + contract(hidden_up[1, :, at], masked[:, WIDE:], (0, 0))
        to = pl.ds(pl.multiple_of(D + index * TILE, TILE), TILE)
        grads[to, :] = total.astype(jnp.bfloat16)

    tiles(WIDE, TILE, down)
    move_rows(spans_out, unit, grads_out, grads, sem.at[1], False)
    pltpu.make_async_copy(grads, grads, sem.at[1]).wait()


def rows_kernel(spans_in, unit, kept, dz_ref, *refs):
    arrived = refs[:len(spans_in)]
    out_ref, weights, sem = refs[len(spans_in) + kept:]
    move_rows(spans_in, unit, arrived, weights, sem.at[0], True)
    pltpu.make_async_copy(weights, weights, sem.at[0]).wait()

    def one(at, index):
        out_ref[:, at] = contract(dz_ref[...], weights[at, :], (1, 1)).astype(jnp.bfloat16)

    tiles(D, TILE, one)


def slot_backward(step, spans_in, spans_out, unit, token_rows, cotangents, live_count, arrived):
    devices, cap = arrived[0].shape[0], token_rows.shape[3]
    rows = devices * CHUNKS * unit
    mine = pl.BlockSpec((None, None, None, cap, D), lambda i: (step, 0, 0, 0, 0))
    any_spec = pl.BlockSpec(memory_space=pl.ANY)
    out = pl.pallas_call(
        functools.partial(slot_kernel, spans_in, spans_out, unit),
        grid=(1,),
        in_specs=[pl.BlockSpec(memory_space=pltpu.SMEM), mine, mine] + [any_spec] * len(arrived),
        out_specs=[any_spec] * len(spans_out) + [pl.BlockSpec((cap, WIDE), lambda i: (0, 0))],
        out_shape=[
            jax.ShapeDtypeStruct((devices, count * unit, WIDE), jnp.bfloat16)
            for _, count in spans_out
        ]
        + [jax.ShapeDtypeStruct((cap, WIDE), jnp.bfloat16)],
        scratch_shapes=[
            pltpu.VMEM((rows, WIDE), jnp.bfloat16),
            pltpu.VMEM((rows, WIDE), jnp.bfloat16),
            pltpu.VMEM((cap, D), jnp.bfloat16),
            pltpu.VMEM((cap, WIDE), jnp.float32),
            pltpu.VMEM((2, FF, WIDE), jnp.bfloat16),
            pltpu.VMEM((cap, FF), jnp.bfloat16),
            pltpu.VMEM((2, cap, WIDE), jnp.bfloat16),
            pltpu.SemaphoreType.DMA((2,)),
        ],
        name="slot",
    )(live_count, token_rows, cotangents, *arrived)
    return out[:-1], out[-1]


def row_grads(step, spans_in, unit, pre_grad, arrived, shape, before):
    devices, cap = arrived[0].shape[0], pre_grad.shape[0]
    rows = devices * CHUNKS * unit
    kept = [] if before is None else [before]
    any_spec = pl.BlockSpec(memory_space=pl.ANY)
    return pl.pallas_call(
        functools.partial(rows_kernel, spans_in, unit, len(kept)),
        grid=(1,),
        in_specs=[pl.BlockSpec((cap, WIDE), lambda i: (0, 0))] + [any_spec] * (len(arrived) + len(kept)),
        out_specs=pl.BlockSpec((None, None, None, cap, D), lambda i: (step, 0, 0, 0, 0)),
        out_shape=jax.ShapeDtypeStruct(shape, jnp.bfloat16),
        scratch_shapes=[pltpu.VMEM((rows, WIDE), jnp.bfloat16), pltpu.SemaphoreType.DMA((1,))],
        input_output_aliases={1 + len(arrived): 0} if kept else {},
        name="rows",
    )(pre_grad, *arrived, *kept)


def pack_out(experts, rows, ids_ref, staged, out_ref):
    span = experts * rows

    def one(dest, carry):
        base = ids_ref[dest] * rows
        for lane in range(WIDE // LANES):
            piece = staged[pl.ds(pl.multiple_of(lane * span + base, 8), rows), :]
            out_ref[dest, :, lane * LANES:(lane + 1) * LANES] = piece.astype(jnp.bfloat16)
        return carry

    lax.fori_loop(0, out_ref.shape[0], one, 0)


def pack_kernel(experts, rows, ids_ref, w_ref, out_ref, staged):
    span = experts * rows
    for row in range(rows):
        for lane in range(WIDE // LANES):
            at = row * WIDE + lane * LANES
            staged[pl.ds(lane * span + row, experts, stride=rows), :] = w_ref[:, at:at + LANES]
    pack_out(experts, rows, ids_ref, staged, out_ref)


def sophia_kernel(experts, rows, packs, kept, *refs):
    ids_ref, next_ref, got_ref, m_ref, c_ref, w_ref = refs[:6]
    refs = refs[6 + kept:]
    m_out, c_out, w_out = refs[:3]
    total = refs[-1]
    span = experts * rows
    total[...] = jnp.zeros_like(total)

    def add(source, carry):
        base = ids_ref[source] * rows
        for lane in range(WIDE // LANES):
            at = pl.ds(pl.multiple_of(lane * span + base, 8), rows)
            piece = got_ref[source, :, lane * LANES:(lane + 1) * LANES]
            total[at, :] = total[at, :] + piece.astype(jnp.float32)
        return carry

    lax.fori_loop(0, got_ref.shape[0], add, 0)
    for row in range(rows):
        for lane in range(WIDE // LANES):
            at = pl.ds(lane * span + row, experts, stride=rows)
            cols = pl.ds(row * WIDE + lane * LANES, LANES)
            grads = total[at, :] * grad_scale
            moment = beta_one * m_ref[:, cols] + (1.0 - beta_one) * grads
            curve = beta_two * c_ref[:, cols] + (1.0 - beta_two) * grads * grads
            weight = w_ref[:, cols] - learn_rate * jnp.clip(
                moment / (rho_scale * curve), -1.0, 1.0
            )
            m_out[:, cols] = moment
            c_out[:, cols] = curve
            w_out[:, cols] = weight
            if packs:
                total[at, :] = weight
    if packs:
        pack_out(experts, rows, next_ref, total, refs[3])


def block_rows(chunk_rows):
    return 16 if chunk_rows % 16 == 0 else chunk_rows


def pack_chunk(span, unit, ids, master):
    experts, devices = master.shape[0], ids.shape[0]
    rows = block_rows(unit)
    chunk_rows = span[1] * unit
    steps = chunk_rows // rows
    shift = span[0] * unit // rows
    return pl.pallas_call(
        functools.partial(pack_kernel, experts, rows),
        grid_spec=pltpu.PrefetchScalarGridSpec(
            num_scalar_prefetch=1,
            grid=(steps,),
            in_specs=[pl.BlockSpec((experts, rows * WIDE), lambda i, *_: (0, shift + i))],
            out_specs=pl.BlockSpec((devices, rows, WIDE), lambda i, *_: (0, i, 0)),
            scratch_shapes=[pltpu.VMEM((WIDE // LANES * experts * rows, LANES), jnp.float32)],
        ),
        out_shape=jax.ShapeDtypeStruct((devices, chunk_rows, WIDE), jnp.bfloat16),
        name="pack",
    )(ids, master)


def sophia_chunk(span, unit, ids, next_ids, got, state, whole, final):
    experts, devices = state[0].shape[0], ids.shape[0]
    rows = block_rows(unit)
    chunk_rows = span[1] * unit
    steps = chunk_rows // rows
    shift = span[0] * unit // rows
    kept = 0 if whole is None else 3
    near = pl.BlockSpec((experts, rows * WIDE), lambda i, *_: (0, i))
    far = pl.BlockSpec((experts, rows * WIDE), lambda i, *_: (0, shift + i))
    packed = pl.BlockSpec((devices, rows, WIDE), lambda i, *_: (0, i, 0))
    width = unit * CHUNKS * WIDE if final else chunk_rows * WIDE
    out_shape = [jax.ShapeDtypeStruct((experts, width), jnp.float32)] * 3
    out_specs = [far if final else near] * 3
    if not final:
        out_shape = out_shape + [jax.ShapeDtypeStruct((devices, chunk_rows, WIDE), jnp.bfloat16)]
        out_specs = out_specs + [packed]
    return pl.pallas_call(
        functools.partial(sophia_kernel, experts, rows, not final, kept),
        grid_spec=pltpu.PrefetchScalarGridSpec(
            num_scalar_prefetch=2,
            grid=(steps,),
            in_specs=[packed]
            + [near if final else far] * 3
            + [pl.BlockSpec(memory_space=pl.ANY)] * kept,
            out_specs=out_specs,
            scratch_shapes=[pltpu.VMEM((WIDE // LANES * experts * rows, LANES), jnp.float32)],
        ),
        out_shape=out_shape,
        input_output_aliases={6 + i: i for i in range(kept)},
        name="sophia",
    )(ids, next_ids, got, *state, *(whole or ()))


def body(token_rows, cotangents, row_counts, old_place, new_place, momentum, curvature, master):
    group_count = lax.axis_size("grp")
    slot_count = lax.axis_size("slot")
    device_count = group_count * slot_count
    experts = master.shape[0]
    per_group = experts // group_count
    unit = master.shape[1] // (CHUNKS * WIDE)
    owners = (jnp.arange(group_count, dtype=jnp.int32) * per_group)[None, :]
    ids = [(place + owners).reshape(-1) for place in (old_place, new_place)]

    def swap(array):
        return lax.all_to_all(array, ("slot", "grp"), split_axis=0, concat_axis=0, tiled=True)

    spans = FIRST
    arrived = [swap(pack_chunk(span, unit, ids[0], master)) for span in spans]
    rows_out = None
    states = [(momentum, curvature, master)] * len(REST)
    whole = None
    for step in range(2):
        final = step == 1
        grads, pre_grad = slot_backward(
            step, spans, REST, unit, token_rows, cotangents, row_counts[step, 0], arrived
        )
        got = [swap(part) for part in grads]
        rows_out = row_grads(
            step, spans, unit, pre_grad, arrived, token_rows.shape, rows_out
        )
        spans, arrived = REST, []
        for k, span in enumerate(REST):
            result = sophia_chunk(span, unit, ids[step], ids[1], got[k], states[k], whole, final)
            if final:
                whole = tuple(result)
            else:
                states[k] = tuple(result[:3])
                arrived.append(swap(result[3]))
    return (rows_out, *whole)


def solution(mesh):
    return jax.shard_map(
        body,
        mesh=mesh,
        in_specs=(
            P(None, "slot", "grp", None, None),
            P(None, "slot", "grp", None, None),
            P(None, "slot", "grp"),
            P(),
            P(),
            P(None, ("slot", "grp")),
            P(None, ("slot", "grp")),
            P(None, ("slot", "grp")),
        ),
        out_specs=(
            P(None, "slot", "grp", None, None),
            P(None, ("slot", "grp")),
            P(None, ("slot", "grp")),
            P(None, ("slot", "grp")),
        ),
        check_vma=False,
    )
```

```python
import functools

import jax
import jax.numpy as jnp
from jax import lax
from jax.experimental import pallas as pl
from jax.experimental.pallas import tpu as pltpu
from jax.sharding import PartitionSpec as P

D = 2048
FF = 512
WIDE = 2 * FF
LANES = 128
TILE = 256
CHUNKS = 3
FIRST = ((0, 1), (1, 2))
REST = ((0, 2), (2, 1))


beta_one = 0.9
beta_two = 0.99
rho_scale = 2.0
learn_rate = 0.005
grad_scale = 0.25


def silu_parts(values):
    sigmoid = jax.nn.sigmoid(values)
    return (values * sigmoid, sigmoid * (1.0 + values * (1.0 - sigmoid)))


def contract(left, right, dims):
    return lax.dot_general(left, right, ((dims[:1], dims[1:]), ((), ())), preferred_element_type=jnp.float32)


def move_rows(spans, unit, chunk_refs, whole, sem, inward, low, high):
    share = whole.shape[0] // chunk_refs[0].shape[0]
    for (start, count), ref in zip(spans, chunk_refs):
        rows = count * unit

        def one(device, carry):
            part = whole.at[pl.ds(pl.multiple_of(device * share + start * unit, 8), rows), :]
            ends = (ref.at[device], part) if inward else (part, ref.at[device])
            pltpu.make_async_copy(*ends, sem).start()
            return carry

        lax.fori_loop(low, high, one, 0)


def await_rows(whole, low, high, sem):
    part = whole.at[low:high, :]
    pltpu.make_async_copy(part, part, sem).wait()


def spread(half):
    row = lax.broadcasted_iota(jnp.int32, (TILE // 2, TILE), 0)
    column = lax.broadcasted_iota(jnp.int32, (TILE // 2, TILE), 1)
    return jnp.where(column == 2 * row + half, 1.0, 0.0).astype(jnp.bfloat16)


def tiles(extent, size, step):
    def one(index, carry):
        step(pl.ds(pl.multiple_of(index * size, size), size), index)
        return carry

    lax.fori_loop(0, extent // size, one, 0)


def slot_kernel(step, spans_in, spans_out, unit, count_ref, x_in, ct_in, *refs):
    n_in, n_out = len(spans_in), len(spans_out)
    arrived, refs = refs[:n_in], refs[n_in:]
    grads_out, refs = refs[:n_out], refs[n_out:]
    dz, weights, grads, x_ref, masked, preact, halves, hidden, hidden_up, sem = refs
    devices = arrived[0].shape[0]
    share = weights.shape[0] // devices
    early = pl.cdiv(D, share)
    ct_copy = pltpu.make_async_copy(ct_in.at[step, 0, 0], masked, sem.at[2])
    x_copy = pltpu.make_async_copy(x_in.at[step, 0, 0], x_ref, sem.at[3])
    ct_copy.start()
    x_copy.start()
    move_rows(spans_in, unit, arrived, weights, sem.at[0], True, 0, early)
    move_rows(spans_in, unit, arrived, weights, sem.at[4], True, early, devices)
    live_count = count_ref[0]
    ct_copy.wait()

    def mask(at, index):
        values = masked[at, :].astype(jnp.float32)
        row = index * 16 + lax.broadcasted_iota(jnp.int32, values.shape, 0)
        masked[at, :] = jnp.where(row < live_count, values, 0.0).astype(jnp.bfloat16)

    tiles(masked.shape[0], 16, mask)
    x_copy.wait()
    await_rows(weights, 0, early * share, sem.at[0])

    def forward(at, index):
        preact[:, at] = contract(x_ref[...], weights[:D, at], (1, 0))

    tiles(WIDE, TILE, forward)
    await_rows(weights, early * share, devices * share, sem.at[4])

    def split(at, index):
        part = weights[pl.ds(pl.multiple_of(D + index * TILE, TILE), TILE), :]
        to = pl.ds(pl.multiple_of(index * (TILE // 2), TILE // 2), TILE // 2)
        for half in range(2):
            halves[half, to, :] = contract(spread(half), part, (1, 0)).astype(jnp.bfloat16)

    tiles(WIDE, TILE, split)

    def backward(at, index):
        hidden_grad = contract(masked[:, :WIDE], halves[0, at, :], (1, 1))
        hidden_grad = hidden_grad + contract(masked[:, WIDE:], halves[1, at, :], (1, 1))
        up_at = pl.ds(pl.multiple_of(FF + index * TILE, TILE), TILE)
        up_pre = preact[:, up_at]
        activated, slope = silu_parts(preact[:, at])
        hidden[:, at] = (activated * up_pre).astype(jnp.bfloat16)
        dz[:, at] = (hidden_grad * up_pre * slope).astype(jnp.bfloat16)
        dz[:, up_at] = (hidden_grad * activated).astype(jnp.bfloat16)

    tiles(FF, TILE, backward)

    def widen(at, index):
        part = hidden[:, pl.ds(pl.multiple_of(index * (TILE // 2), TILE // 2), TILE // 2)]
        for half in range(2):
            hidden_up[half, :, at] = contract(part, spread(half), (1, 0)).astype(jnp.bfloat16)

    tiles(WIDE, TILE, widen)

    def send(index):
        low, high = index * TILE // share, (index + 1) * TILE // share
        move_rows(spans_out, unit, grads_out, grads, sem.at[1], False, low, high)

    def gateup(at, index):
        grads[at, :] = contract(x_ref[:, at], dz[...], (0, 0)).astype(jnp.bfloat16)
        send(index)

    tiles(D, TILE, gateup)

    def down(at, index):
        total = contract(hidden_up[0, :, at], masked[:, :WIDE], (0, 0))
        total = total + contract(hidden_up[1, :, at], masked[:, WIDE:], (0, 0))
        to = pl.ds(pl.multiple_of(D + index * TILE, TILE), TILE)
        grads[to, :] = total.astype(jnp.bfloat16)
        send(D // TILE + index)

    tiles(WIDE, TILE, down)
    pltpu.make_async_copy(grads, grads, sem.at[1]).wait()


def rows_kernel(spans_in, unit, kept, dz_ref, *refs):
    arrived = refs[:len(spans_in)]
    out_ref, weights, sem = refs[len(spans_in) + kept:]
    early = pl.cdiv(D, weights.shape[0] // arrived[0].shape[0])
    share = weights.shape[0] // arrived[0].shape[0]
    move_rows(spans_in, unit, arrived, weights, sem.at[0], True, 0, early)
    await_rows(weights, 0, early * share, sem.at[0])

    def one(at, index):
        out_ref[:, at] = contract(dz_ref[...], weights[at, :], (1, 1)).astype(jnp.bfloat16)

    tiles(D, TILE, one)


def slot_backward(step, spans_in, spans_out, unit, token_rows, cotangents, live_count, arrived):
    devices, cap = arrived[0].shape[0], token_rows.shape[3]
    rows = devices * CHUNKS * unit
    any_spec = pl.BlockSpec(memory_space=pl.ANY)
    out = pl.pallas_call(
        functools.partial(slot_kernel, step, spans_in, spans_out, unit),
        grid=(1,),
        in_specs=[pl.BlockSpec(memory_space=pltpu.SMEM)] + [any_spec] * (2 + len(arrived)),
        out_specs=[any_spec] * len(spans_out) + [pl.BlockSpec((cap, WIDE), lambda i: (0, 0))],
        out_shape=[
            jax.ShapeDtypeStruct((devices, count * unit, WIDE), jnp.bfloat16)
            for _, count in spans_out
        ]
        + [jax.ShapeDtypeStruct((cap, WIDE), jnp.bfloat16)],
        scratch_shapes=[
            pltpu.VMEM((rows, WIDE), jnp.bfloat16),
            pltpu.VMEM((rows, WIDE), jnp.bfloat16),
            pltpu.VMEM((cap, D), jnp.bfloat16),
            pltpu.VMEM((cap, D), jnp.bfloat16),
            pltpu.VMEM((cap, WIDE), jnp.float32),
            pltpu.VMEM((2, FF, WIDE), jnp.bfloat16),
            pltpu.VMEM((cap, FF), jnp.bfloat16),
            pltpu.VMEM((2, cap, WIDE), jnp.bfloat16),
            pltpu.SemaphoreType.DMA((5,)),
        ],
        name="slot",
    )(live_count, token_rows, cotangents, *arrived)
    return out[:-1], out[-1]


def row_grads(step, spans_in, unit, pre_grad, arrived, shape, before):
    devices, cap = arrived[0].shape[0], pre_grad.shape[0]
    rows = devices * CHUNKS * unit
    kept = [] if before is None else [before]
    any_spec = pl.BlockSpec(memory_space=pl.ANY)
    return pl.pallas_call(
        functools.partial(rows_kernel, spans_in, unit, len(kept)),
        grid=(1,),
        in_specs=[pl.BlockSpec((cap, WIDE), lambda i: (0, 0))] + [any_spec] * (len(arrived) + len(kept)),
        out_specs=pl.BlockSpec((None, None, None, cap, D), lambda i: (step, 0, 0, 0, 0)),
        out_shape=jax.ShapeDtypeStruct(shape, jnp.bfloat16),
        scratch_shapes=[pltpu.VMEM((rows, WIDE), jnp.bfloat16), pltpu.SemaphoreType.DMA((1,))],
        input_output_aliases={1 + len(arrived): 0} if kept else {},
        name="rows",
    )(pre_grad, *arrived, *kept)


def pack_out(experts, rows, ids_ref, staged, out_ref):
    span = experts * rows

    def one(dest, carry):
        base = ids_ref[dest] * rows
        for lane in range(WIDE // LANES):
            piece = staged[pl.ds(pl.multiple_of(lane * span + base, 8), rows), :]
            out_ref[dest, :, lane * LANES:(lane + 1) * LANES] = piece.astype(jnp.bfloat16)
        return carry

    lax.fori_loop(0, out_ref.shape[0], one, 0)


def pack_kernel(experts, rows, ids_ref, w_ref, out_ref, staged):
    span = experts * rows
    for row in range(rows):
        for lane in range(WIDE // LANES):
            at = row * WIDE + lane * LANES
            staged[pl.ds(lane * span + row, experts, stride=rows), :] = w_ref[:, at:at + LANES]
    pack_out(experts, rows, ids_ref, staged, out_ref)


def sophia_kernel(experts, rows, packs, kept, *refs):
    ids_ref, next_ref, got_ref, m_ref, c_ref, w_ref = refs[:6]
    refs = refs[6 + kept:]
    m_out, c_out, w_out = refs[:3]
    total = refs[-1]
    span = experts * rows
    total[...] = jnp.zeros_like(total)

    def add(source, carry):
        base = ids_ref[source] * rows
        for lane in range(WIDE // LANES):
            at = pl.ds(pl.multiple_of(lane * span + base, 8), rows)
            piece = got_ref[source, :, lane * LANES:(lane + 1) * LANES]
            total[at, :] = total[at, :] + piece.astype(jnp.float32)
        return carry

    lax.fori_loop(0, got_ref.shape[0], add, 0)
    for row in range(rows):
        for lane in range(WIDE // LANES):
            at = pl.ds(lane * span + row, experts, stride=rows)
            cols = pl.ds(row * WIDE + lane * LANES, LANES)
            grads = total[at, :] * grad_scale
            moment = beta_one * m_ref[:, cols] + (1.0 - beta_one) * grads
            curve = beta_two * c_ref[:, cols] + (1.0 - beta_two) * grads * grads
            weight = w_ref[:, cols] - learn_rate * jnp.clip(
                moment / (rho_scale * curve), -1.0, 1.0
            )
            m_out[:, cols] = moment
            c_out[:, cols] = curve
            w_out[:, cols] = weight
            if packs:
                total[at, :] = weight
    if packs:
        pack_out(experts, rows, next_ref, total, refs[3])


def block_rows(chunk_rows):
    return 16 if chunk_rows % 16 == 0 else chunk_rows


def pack_chunk(span, unit, ids, master):
    experts, devices = master.shape[0], ids.shape[0]
    rows = block_rows(unit)
    chunk_rows = span[1] * unit
    steps = chunk_rows // rows
    shift = span[0] * unit // rows
    return pl.pallas_call(
        functools.partial(pack_kernel, experts, rows),
        grid_spec=pltpu.PrefetchScalarGridSpec(
            num_scalar_prefetch=1,
            grid=(steps,),
            in_specs=[pl.BlockSpec((experts, rows * WIDE), lambda i, *_: (0, shift + i))],
            out_specs=pl.BlockSpec((devices, rows, WIDE), lambda i, *_: (0, i, 0)),
            scratch_shapes=[pltpu.VMEM((WIDE // LANES * experts * rows, LANES), jnp.float32)],
        ),
        out_shape=jax.ShapeDtypeStruct((devices, chunk_rows, WIDE), jnp.bfloat16),
        name="pack",
    )(ids, master)


def sophia_chunk(span, unit, ids, next_ids, got, state, whole, final):
    experts, devices = state[0].shape[0], ids.shape[0]
    rows = block_rows(unit)
    chunk_rows = span[1] * unit
    steps = chunk_rows // rows
    shift = span[0] * unit // rows
    kept = 0 if whole is None else 3
    near = pl.BlockSpec((experts, rows * WIDE), lambda i, *_: (0, i))
    far = pl.BlockSpec((experts, rows * WIDE), lambda i, *_: (0, shift + i))
    packed = pl.BlockSpec((devices, rows, WIDE), lambda i, *_: (0, i, 0))
    width = unit * CHUNKS * WIDE if final else chunk_rows * WIDE
    out_shape = [jax.ShapeDtypeStruct((experts, width), jnp.float32)] * 3
    out_specs = [far if final else near] * 3
    if not final:
        out_shape = out_shape + [jax.ShapeDtypeStruct((devices, chunk_rows, WIDE), jnp.bfloat16)]
        out_specs = out_specs + [packed]
    return pl.pallas_call(
        functools.partial(sophia_kernel, experts, rows, not final, kept),
        grid_spec=pltpu.PrefetchScalarGridSpec(
            num_scalar_prefetch=2,
            grid=(steps,),
            in_specs=[packed]
            + [near if final else far] * 3
            + [pl.BlockSpec(memory_space=pl.ANY)] * kept,
            out_specs=out_specs,
            scratch_shapes=[pltpu.VMEM((WIDE // LANES * experts * rows, LANES), jnp.float32)],
        ),
        out_shape=out_shape,
        input_output_aliases={6 + i: i for i in range(kept)},
        name="sophia",
    )(ids, next_ids, got, *state, *(whole or ()))


def body(token_rows, cotangents, row_counts, old_place, new_place, momentum, curvature, master):
    group_count = lax.axis_size("grp")
    slot_count = lax.axis_size("slot")
    device_count = group_count * slot_count
    experts = master.shape[0]
    per_group = experts // group_count
    unit = master.shape[1] // (CHUNKS * WIDE)
    owners = (jnp.arange(group_count, dtype=jnp.int32) * per_group)[None, :]
    ids = [(place + owners).reshape(-1) for place in (old_place, new_place)]

    def swap(array):
        return lax.all_to_all(array, ("slot", "grp"), split_axis=0, concat_axis=0, tiled=True)

    spans = FIRST
    arrived = [swap(pack_chunk(span, unit, ids[0], master)) for span in spans]
    rows_out = None
    states = [(momentum, curvature, master)] * len(REST)
    whole = None
    for step in range(2):
        final = step == 1
        grads, pre_grad = slot_backward(
            step, spans, REST, unit, token_rows, cotangents, row_counts[step, 0], arrived
        )
        got = [swap(part) for part in grads]
        rows_out = row_grads(
            step, spans, unit, pre_grad, arrived, token_rows.shape, rows_out
        )
        spans, arrived = REST, []
        for k, span in enumerate(REST):
            result = sophia_chunk(span, unit, ids[step], ids[1], got[k], states[k], whole, final)
            if final:
                whole = tuple(result)
            else:
                states[k] = tuple(result[:3])
                arrived.append(swap(result[3]))
    return (rows_out, *whole)


def solution(mesh):
    return jax.shard_map(
        body,
        mesh=mesh,
        in_specs=(
            P(None, "slot", "grp", None, None),
            P(None, "slot", "grp", None, None),
            P(None, "slot", "grp"),
            P(),
            P(),
            P(None, ("slot", "grp")),
            P(None, ("slot", "grp")),
            P(None, ("slot", "grp")),
        ),
        out_specs=(
            P(None, "slot", "grp", None, None),
            P(None, ("slot", "grp")),
            P(None, ("slot", "grp")),
            P(None, ("slot", "grp")),
        ),
        check_vma=False,
    )
```

```python
import functools

import jax
import jax.numpy as jnp
from jax import lax
from jax.experimental import pallas as pl
from jax.experimental.pallas import tpu as pltpu
from jax.sharding import PartitionSpec as P

D = 2048
FF = 512
WIDE = 2 * FF
LANES = 128
TILE = 256


beta_one = 0.9
beta_two = 0.99
rho_scale = 2.0
learn_rate = 0.005
grad_scale = 0.25


def silu_parts(values):
    sigmoid = jax.nn.sigmoid(values)
    return (values * sigmoid, sigmoid * (1.0 + values * (1.0 - sigmoid)))


def contract(left, right, dims):
    return lax.dot_general(left, right, ((dims[:1], dims[1:]), ((), ())), preferred_element_type=jnp.float32)


def move_rows(spans, unit, chunk_refs, whole, sem, inward, low, high):
    share = whole.shape[0] // chunk_refs[0].shape[0]
    for (start, count), ref in zip(spans, chunk_refs):
        rows = count * unit

        def one(device, carry):
            part = whole.at[pl.ds(pl.multiple_of(device * share + start * unit, 8), rows), :]
            ends = (ref.at[device], part) if inward else (part, ref.at[device])
            pltpu.make_async_copy(*ends, sem).start()
            return carry

        lax.fori_loop(low, high, one, 0)


def await_rows(whole, low, high, sem):
    part = whole.at[low:high, :]
    pltpu.make_async_copy(part, part, sem).wait()


def spread(half):
    row = lax.broadcasted_iota(jnp.int32, (TILE // 2, TILE), 0)
    column = lax.broadcasted_iota(jnp.int32, (TILE // 2, TILE), 1)
    return jnp.where(column == 2 * row + half, 1.0, 0.0).astype(jnp.bfloat16)


def tiles(extent, size, step):
    def one(index, carry):
        step(pl.ds(pl.multiple_of(index * size, size), size), index)
        return carry

    lax.fori_loop(0, extent // size, one, 0)


def slot_kernel(step, spans_in, spans_out, unit, count_ref, x_in, ct_in, *refs):
    n_in, n_out = len(spans_in), len(spans_out)
    arrived, refs = refs[:n_in], refs[n_in:]
    grads_out, refs = refs[:n_out], refs[n_out:]
    dz, weights, grads, x_ref, masked, preact, halves, hidden, hidden_up, sem = refs
    devices = arrived[0].shape[0]
    share = weights.shape[0] // devices
    early = pl.cdiv(D, share)
    ct_copy = pltpu.make_async_copy(ct_in.at[step, 0, 0], masked, sem.at[2])
    x_copy = pltpu.make_async_copy(x_in.at[step, 0, 0], x_ref, sem.at[3])
    ct_copy.start()
    x_copy.start()
    move_rows(spans_in, unit, arrived, weights, sem.at[0], True, 0, early)
    move_rows(spans_in, unit, arrived, weights, sem.at[4], True, early, devices)
    live_count = count_ref[0]
    ct_copy.wait()

    def mask(at, index):
        values = masked[at, :].astype(jnp.float32)
        row = index * 16 + lax.broadcasted_iota(jnp.int32, values.shape, 0)
        masked[at, :] = jnp.where(row < live_count, values, 0.0).astype(jnp.bfloat16)

    tiles(masked.shape[0], 16, mask)
    x_copy.wait()
    await_rows(weights, 0, early * share, sem.at[0])

    def forward(at, index):
        preact[:, at] = contract(x_ref[...], weights[:D, at], (1, 0))

    tiles(WIDE, TILE, forward)
    await_rows(weights, early * share, devices * share, sem.at[4])

    def split(at, index):
        part = weights[pl.ds(pl.multiple_of(D + index * TILE, TILE), TILE), :]
        to = pl.ds(pl.multiple_of(index * (TILE // 2), TILE // 2), TILE // 2)
        for half in range(2):
            halves[half, to, :] = contract(spread(half), part, (1, 0)).astype(jnp.bfloat16)

    tiles(WIDE, TILE, split)

    def backward(at, index):
        hidden_grad = contract(masked[:, :WIDE], halves[0, at, :], (1, 1))
        hidden_grad = hidden_grad + contract(masked[:, WIDE:], halves[1, at, :], (1, 1))
        up_at = pl.ds(pl.multiple_of(FF + index * TILE, TILE), TILE)
        up_pre = preact[:, up_at]
        activated, slope = silu_parts(preact[:, at])
        hidden[:, at] = (activated * up_pre).astype(jnp.bfloat16)
        dz[:, at] = (hidden_grad * up_pre * slope).astype(jnp.bfloat16)
        dz[:, up_at] = (hidden_grad * activated).astype(jnp.bfloat16)

    tiles(FF, TILE, backward)

    def widen(at, index):
        part = hidden[:, pl.ds(pl.multiple_of(index * (TILE // 2), TILE // 2), TILE // 2)]
        for half in range(2):
            hidden_up[half, :, at] = contract(part, spread(half), (1, 0)).astype(jnp.bfloat16)

    tiles(WIDE, TILE, widen)

    def send(index):
        low, high = index * TILE // share, (index + 1) * TILE // share
        move_rows(spans_out, unit, grads_out, grads, sem.at[1], False, low, high)

    def gateup(at, index):
        grads[at, :] = contract(x_ref[:, at], dz[...], (0, 0)).astype(jnp.bfloat16)
        send(index)

    tiles(D, TILE, gateup)

    def down(at, index):
        total = contract(hidden_up[0, :, at], masked[:, :WIDE], (0, 0))
        total = total + contract(hidden_up[1, :, at], masked[:, WIDE:], (0, 0))
        to = pl.ds(pl.multiple_of(D + index * TILE, TILE), TILE)
        grads[to, :] = total.astype(jnp.bfloat16)
        send(D // TILE + index)

    tiles(WIDE, TILE, down)
    pltpu.make_async_copy(grads, grads, sem.at[1]).wait()


def rows_kernel(spans_in, unit, kept, dz_ref, *refs):
    arrived = refs[:len(spans_in)]
    out_ref, weights, sem = refs[len(spans_in) + kept:]
    early = pl.cdiv(D, weights.shape[0] // arrived[0].shape[0])
    share = weights.shape[0] // arrived[0].shape[0]
    move_rows(spans_in, unit, arrived, weights, sem.at[0], True, 0, early)
    await_rows(weights, 0, early * share, sem.at[0])

    def one(at, index):
        out_ref[:, at] = contract(dz_ref[...], weights[at, :], (1, 1)).astype(jnp.bfloat16)

    tiles(D, TILE, one)


def slot_backward(step, spans_in, spans_out, unit, token_rows, cotangents, live_count, arrived):
    devices, cap = arrived[0].shape[0], token_rows.shape[3]
    rows = devices * unit * sum(count for _, count in spans_in)
    any_spec = pl.BlockSpec(memory_space=pl.ANY)
    out = pl.pallas_call(
        functools.partial(slot_kernel, step, spans_in, spans_out, unit),
        grid=(1,),
        in_specs=[pl.BlockSpec(memory_space=pltpu.SMEM)] + [any_spec] * (2 + len(arrived)),
        out_specs=[any_spec] * len(spans_out) + [pl.BlockSpec((cap, WIDE), lambda i: (0, 0))],
        out_shape=[
            jax.ShapeDtypeStruct((devices, count * unit, WIDE), jnp.bfloat16)
            for _, count in spans_out
        ]
        + [jax.ShapeDtypeStruct((cap, WIDE), jnp.bfloat16)],
        scratch_shapes=[
            pltpu.VMEM((rows, WIDE), jnp.bfloat16),
            pltpu.VMEM((rows, WIDE), jnp.bfloat16),
            pltpu.VMEM((cap, D), jnp.bfloat16),
            pltpu.VMEM((cap, D), jnp.bfloat16),
            pltpu.VMEM((cap, WIDE), jnp.float32),
            pltpu.VMEM((2, FF, WIDE), jnp.bfloat16),
            pltpu.VMEM((cap, FF), jnp.bfloat16),
            pltpu.VMEM((2, cap, WIDE), jnp.bfloat16),
            pltpu.SemaphoreType.DMA((5,)),
        ],
        name="slot",
    )(live_count, token_rows, cotangents, *arrived)
    return out[:-1], out[-1]


def row_grads(step, spans_in, unit, pre_grad, arrived, shape, before):
    devices, cap = arrived[0].shape[0], pre_grad.shape[0]
    rows = devices * unit * sum(count for _, count in spans_in)
    kept = [] if before is None else [before]
    any_spec = pl.BlockSpec(memory_space=pl.ANY)
    return pl.pallas_call(
        functools.partial(rows_kernel, spans_in, unit, len(kept)),
        grid=(1,),
        in_specs=[pl.BlockSpec((cap, WIDE), lambda i: (0, 0))] + [any_spec] * (len(arrived) + len(kept)),
        out_specs=pl.BlockSpec((None, None, None, cap, D), lambda i: (step, 0, 0, 0, 0)),
        out_shape=jax.ShapeDtypeStruct(shape, jnp.bfloat16),
        scratch_shapes=[pltpu.VMEM((rows, WIDE), jnp.bfloat16), pltpu.SemaphoreType.DMA((1,))],
        input_output_aliases={1 + len(arrived): 0} if kept else {},
        name="rows",
    )(pre_grad, *arrived, *kept)


def pack_out(experts, rows, ids_ref, staged, out_ref):
    span = experts * rows

    def one(dest, carry):
        base = ids_ref[dest] * rows
        for lane in range(WIDE // LANES):
            piece = staged[pl.ds(pl.multiple_of(lane * span + base, 8), rows), :]
            out_ref[dest, :, lane * LANES:(lane + 1) * LANES] = piece.astype(jnp.bfloat16)
        return carry

    lax.fori_loop(0, out_ref.shape[0], one, 0)


def pack_kernel(experts, rows, ids_ref, w_ref, out_ref, staged):
    span = experts * rows
    for row in range(rows):
        for lane in range(WIDE // LANES):
            at = row * WIDE + lane * LANES
            staged[pl.ds(lane * span + row, experts, stride=rows), :] = w_ref[:, at:at + LANES]
    pack_out(experts, rows, ids_ref, staged, out_ref)


def sophia_kernel(experts, rows, packs, kept, *refs):
    ids_ref, next_ref, got_ref, m_ref, c_ref, w_ref = refs[:6]
    refs = refs[6 + kept:]
    m_out, c_out, w_out = refs[:3]
    total = refs[-1]
    span = experts * rows
    total[...] = jnp.zeros_like(total)

    def add(source, carry):
        base = ids_ref[source] * rows
        for lane in range(WIDE // LANES):
            at = pl.ds(pl.multiple_of(lane * span + base, 8), rows)
            piece = got_ref[source, :, lane * LANES:(lane + 1) * LANES]
            total[at, :] = total[at, :] + piece.astype(jnp.float32)
        return carry

    lax.fori_loop(0, got_ref.shape[0], add, 0)
    for row in range(rows):
        for lane in range(WIDE // LANES):
            at = pl.ds(lane * span + row, experts, stride=rows)
            cols = pl.ds(row * WIDE + lane * LANES, LANES)
            grads = total[at, :] * grad_scale
            moment = beta_one * m_ref[:, cols] + (1.0 - beta_one) * grads
            curve = beta_two * c_ref[:, cols] + (1.0 - beta_two) * grads * grads
            weight = w_ref[:, cols] - learn_rate * jnp.clip(
                moment / (rho_scale * curve), -1.0, 1.0
            )
            m_out[:, cols] = moment
            c_out[:, cols] = curve
            w_out[:, cols] = weight
            if packs:
                total[at, :] = weight
    if packs:
        pack_out(experts, rows, next_ref, total, refs[3])


def block_rows(chunk_rows):
    return 16 if chunk_rows % 16 == 0 else chunk_rows


def pack_chunk(span, unit, ids, master):
    experts, devices = master.shape[0], ids.shape[0]
    rows = block_rows(unit)
    chunk_rows = span[1] * unit
    steps = chunk_rows // rows
    shift = span[0] * unit // rows
    return pl.pallas_call(
        functools.partial(pack_kernel, experts, rows),
        grid_spec=pltpu.PrefetchScalarGridSpec(
            num_scalar_prefetch=1,
            grid=(steps,),
            in_specs=[pl.BlockSpec((experts, rows * WIDE), lambda i, *_: (0, shift + i))],
            out_specs=pl.BlockSpec((devices, rows, WIDE), lambda i, *_: (0, i, 0)),
            scratch_shapes=[pltpu.VMEM((WIDE // LANES * experts * rows, LANES), jnp.float32)],
        ),
        out_shape=jax.ShapeDtypeStruct((devices, chunk_rows, WIDE), jnp.bfloat16),
        name="pack",
    )(ids, master)


def sophia_chunk(span, unit, ids, next_ids, got, state, whole, width):
    experts, devices = state[0].shape[0], ids.shape[0]
    rows = block_rows(unit)
    chunk_rows = span[1] * unit
    steps = chunk_rows // rows
    shift = span[0] * unit // rows
    kept = 0 if whole is None else 3
    near = pl.BlockSpec((experts, rows * WIDE), lambda i, *_: (0, i))
    far = pl.BlockSpec((experts, rows * WIDE), lambda i, *_: (0, shift + i))
    packed = pl.BlockSpec((devices, rows, WIDE), lambda i, *_: (0, i, 0))
    final = width is not None
    width = width or chunk_rows * WIDE
    out_shape = [jax.ShapeDtypeStruct((experts, width), jnp.float32)] * 3
    out_specs = [far if final else near] * 3
    if not final:
        out_shape = out_shape + [jax.ShapeDtypeStruct((devices, chunk_rows, WIDE), jnp.bfloat16)]
        out_specs = out_specs + [packed]
    return pl.pallas_call(
        functools.partial(sophia_kernel, experts, rows, not final, kept),
        grid_spec=pltpu.PrefetchScalarGridSpec(
            num_scalar_prefetch=2,
            grid=(steps,),
            in_specs=[packed]
            + [near if final else far] * 3
            + [pl.BlockSpec(memory_space=pl.ANY)] * kept,
            out_specs=out_specs,
            scratch_shapes=[pltpu.VMEM((WIDE // LANES * experts * rows, LANES), jnp.float32)],
        ),
        out_shape=out_shape,
        input_output_aliases={6 + i: i for i in range(kept)},
        name="sophia",
    )(ids, next_ids, got, *state, *(whole or ()))


def body(token_rows, cotangents, row_counts, old_place, new_place, momentum, curvature, master):
    group_count = lax.axis_size("grp")
    slot_count = lax.axis_size("slot")
    device_count = group_count * slot_count
    experts = master.shape[0]
    per_group = experts // group_count
    share = master.shape[1] // WIDE
    unit = 16 if share % 16 == 0 else 8
    parts = share // unit
    rest = ((0, parts - 1), (parts - 1, 1))
    owners = (jnp.arange(group_count, dtype=jnp.int32) * per_group)[None, :]
    ids = [(place + owners).reshape(-1) for place in (old_place, new_place)]

    def swap(array):
        return lax.all_to_all(array, ("slot", "grp"), split_axis=0, concat_axis=0, tiled=True)

    spans = ((0, 1), (1, parts - 1))
    arrived = [swap(pack_chunk(span, unit, ids[0], master)) for span in spans]
    rows_out = None
    states = [(momentum, curvature, master)] * len(rest)
    whole = None
    for step in range(2):
        final = step == 1
        grads, pre_grad = slot_backward(
            step, spans, rest, unit, token_rows, cotangents, row_counts[step, 0], arrived
        )
        got = [swap(part) for part in grads]
        rows_out = row_grads(
            step, spans, unit, pre_grad, arrived, token_rows.shape, rows_out
        )
        spans, arrived = rest, []
        for k, span in enumerate(rest):
            width = master.shape[1] if final else None
            result = sophia_chunk(span, unit, ids[step], ids[1], got[k], states[k], whole, width)
            if final:
                whole = tuple(result)
            else:
                states[k] = tuple(result[:3])
                arrived.append(swap(result[3]))
    return (rows_out, *whole)


def solution(mesh):
    return jax.shard_map(
        body,
        mesh=mesh,
        in_specs=(
            P(None, "slot", "grp", None, None),
            P(None, "slot", "grp", None, None),
            P(None, "slot", "grp"),
            P(),
            P(),
            P(None, ("slot", "grp")),
            P(None, ("slot", "grp")),
            P(None, ("slot", "grp")),
        ),
        out_specs=(
            P(None, "slot", "grp", None, None),
            P(None, ("slot", "grp")),
            P(None, ("slot", "grp")),
            P(None, ("slot", "grp")),
        ),
        check_vma=False,
    )
```
